768 devices in a mesh: wide: 48 (over z, x_hi, core), narrow: 16 (over x_lo, y).
Axes of the slice: x: 4 (x_hi: 2, x_lo: 2; x = x_hi * 2 + x_lo), y: 8, z: 12, core: 2. Of those that a mesh axis runs over, the one named last changes fastest.
Arguments:
- features: bfloat16 [196608, 128], P(('wide', 'narrow')), may hold values from -6 to 6
- block_values: bfloat16 [16, 48, 96, 128, 128], P('narrow', 'wide'), may hold values from -0.125 to 0.125
- block_rows: int32 [16, 48, 96], P('narrow', 'wide'), may hold values from 0 to 95
- block_cols: int32 [16, 48, 96], P('narrow', 'wide'), may hold values from 0 to 31
- counts: int32 [16, 48], P('narrow', 'wide'), may hold values from 1 to 96, as said below
- weight: bfloat16 [128, 256], replicated, may hold values from -0.5 to 0.5
- bias: float32 [256], replicated, may hold values from -3 to 3
Outputs:
- activations: bfloat16 [196608, 256], P(('narrow', 'wide'))
The draws below stay inside these ranges and needn't reach their ends.
Inputs may be any that keep to these rules, and one draw needn't show every extreme that they name: `counts`: each draw has a tile with all 96 slots used.
All inputs are finite; a program needn't handle non-finite values.
Results may differ from the reference program's by a relative error of at most 0.0046.
Values may be sent and summed in bfloat16 or wider, within the bound.
No kernel may reach another device: no remote copies, remote signals or barrier semaphores. Data moves between devices by JAX's collectives and lax.ppermute only.
A program may use at most 64 MiB of HBM per device.

```python
import jax
import jax.numpy as jnp
from jax import lax

F = 128
HID = 256
BLK = 128
ND = 256
KB = 96
NODES = 196608
RBLK = 96
CBLK = 32
N_WIDE = 48
N_NARROW = 16


def draw_counts(key, part):
    first_key, second_key = jax.random.split(jax.random.fold_in(key, 17))
    raw = jax.random.randint(first_key, (N_NARROW * N_WIDE,), 0, KB)
    shaped = 1 + raw * raw // KB
    chosen = jax.random.randint(second_key, (), 0, N_NARROW * N_WIDE)
    filled = jnp.where(jnp.arange(N_NARROW * N_WIDE) == chosen, KB, shaped)
    return filled.reshape(N_NARROW, N_WIDE).astype(jnp.int32)


def plant(values, key, least, high):
    longest = values.shape.index(max(values.shape))
    spots = []
    for shift in (0, 1):
        where = [jax.random.randint(jax.random.fold_in(key, axis), (), 0, length) for axis, length in enumerate(values.shape)]
        where[longest] = (where[longest] + shift) % values.shape[longest]
        spots.append(tuple(where))
    return values.at[spots[0]].set(least).at[spots[1]].set(high)


def levels(rng, dims, cuts, smallest, top_value):
    level = 1.0
    for dim, shards_of in cuts:
        steps = jax.random.uniform(jax.random.fold_in(jax.random.fold_in(rng, 6), dim), (shards_of,), jnp.float32, smallest / len(cuts), top_value / len(cuts))
        level = level * jnp.repeat(jnp.exp(steps), dims[dim] // shards_of).reshape((-1,) + (1,) * (len(dims) - 1 - dim))
    return level


def bell_draw(key, extent, width, reach, shards=(), held_as=jnp.bfloat16):
    factor_of = levels(key, extent, shards, -0.22, 0.18) if shards else 1.0
    values = jax.random.normal(key, extent, jnp.float32) * width * factor_of
    return jnp.minimum(jnp.maximum(values, -reach), reach).astype(held_as)


def setup_inputs(seed: int = 0) -> dict:
    key_list = jax.random.split(jax.random.key(seed), 8)
    features = bell_draw(key_list[0], (NODES, F), 1.0, 6.0, ((0, 768),))
    block_values = bell_draw(key_list[1], (N_NARROW, N_WIDE, KB, BLK, BLK), (BLK * BLK * KB // (3 * ND)) ** -0.5, 0.125, ((0, 16), (1, 48)))
    block_rows = plant(jax.random.randint(key_list[2], (N_NARROW, N_WIDE, KB), 0, RBLK), jax.random.fold_in(key_list[2], 1), 0, RBLK - 1).astype(jnp.int32)
    block_cols = plant(jax.random.randint(key_list[3], (N_NARROW, N_WIDE, KB), 0, CBLK), jax.random.fold_in(key_list[3], 1), 0, CBLK - 1).astype(jnp.int32)
    counts = draw_counts(jax.random.fold_in(key_list[7], 71), 0)
    weight = bell_draw(key_list[5], (F, HID), F ** -0.5, 0.5)
    bias = bell_draw(key_list[6], (HID,), 0.5, 3.0, (), jnp.float32)
    return {"features": features, "block_values": block_values, "block_rows": block_rows, "block_cols": block_cols, "counts": counts, "weight": weight, "bias": bias}


def reference(features, block_values, block_rows, block_cols, counts, weight, bias):
    panel_rows = N_NARROW * ND
    def one_tile(operands):
        values, rows, cols, used, column_panel = operands
        panel_blocks = column_panel.reshape(CBLK, BLK, F)
        picked = panel_blocks[cols.astype(jnp.int32)].astype(jnp.float32)
        products = jnp.einsum("kij,kjf->kif", values.astype(jnp.float32), picked)
        active = (jnp.arange(KB, dtype=jnp.int32) < used).astype(jnp.float32)
        products = products * active[:, None, None]
        summed = jax.ops.segment_sum(products, rows.astype(jnp.int32), num_segments=RBLK)
        return summed.reshape(RBLK * BLK, F)

    def one_panel_row(narrow_index):
        def add_tile(total, wide_index):
            values = block_values[narrow_index, wide_index]
            rows = block_rows[narrow_index, wide_index]
            cols = block_cols[narrow_index, wide_index]
            used = counts[narrow_index, wide_index]
            column_panel = lax.dynamic_slice_in_dim(features, (wide_index * panel_rows).astype(jnp.int32), panel_rows, 0)
            return total + one_tile((values, rows, cols, used, column_panel)), None
        start_total = jnp.zeros((RBLK * BLK, F), jnp.float32)
        total, unused = lax.scan(add_tile, start_total, jnp.arange(N_WIDE, dtype=jnp.int32))
        return total

    aggregated = lax.map(one_panel_row, jnp.arange(N_NARROW, dtype=jnp.int32)).reshape(NODES, F)
    hidden = aggregated.astype(jnp.bfloat16)
    mixed = jnp.dot(hidden, weight, preferred_element_type=jnp.float32) + bias
    return jnp.maximum(mixed, 0.0).astype(jnp.bfloat16)
```

```python
import functools

import jax
import jax.numpy as jnp
from jax import lax
from jax.experimental import pallas as pl
from jax.experimental.pallas import tpu as pltpu
from jax.sharding import PartitionSpec as P

Z, X, CORES, SHARE = 12, 2, 2, 3
RELAYS = Z // SHARE
UNROLL = 8


def wide_index(z, x, core):
    return (z % Z) * (X * CORES) + (x % X) * CORES + core % CORES


def shift(dz=0, dcore=0):
    return [
        (wide_index(z, x, c), wide_index(z + dz, x, c + dcore))
        for z in range(Z) for x in range(X) for c in range(CORES)
    ]


RELAY_GROUPS = [
    [wide_index(SHARE * q + s, x, c) for q in range(RELAYS) for x in range(X)]
    for s in range(SHARE) for c in range(CORES)
]


def place_of(row, place, per_core):
    core = (row // per_core) % CORES
    x = (row // (per_core * CORES)) % X
    z = row // (per_core * CORES * X)
    kept = (core == place[1]).astype(jnp.int32)
    relative = lax.rem(z + SHARE - place[0], SHARE)
    inner = (z // SHARE) * (X * per_core) + x * per_core + row % per_core
    return (kept * SHARE + relative) * (RELAYS * X * per_core) + inner


def tile_sums(used, rows, cols, place, values, panel, sent, kept, total, *, per_core):
    size = values.shape[1]
    slots = values.shape[0]
    half = sent.shape[0]

    def clear(i, carry):
        total[pl.ds(pl.multiple_of(i * size, size), size), :] = jnp.zeros((size, total.shape[1]), jnp.float32)
        return carry

    lax.fori_loop(0, total.shape[0] // size, clear, 0)

    def step(group, carry):
        first = group * UNROLL
        products = []
        for u in range(UNROLL):
            product = jnp.dot(values[first + u], panel[cols[first + u]], preferred_element_type=jnp.float32)
            products.append(jnp.where(first + u < used[0], product, 0.0))
        for u in range(UNROLL):
            at = pl.multiple_of(place_of(rows[first + u], place, per_core) * size, size)
            total[pl.ds(at, size), :] += products[u]
        return carry

    lax.fori_loop(0, (used[0] + UNROLL - 1) // UNROLL, step, 0)

    def give(i, carry):
        at = pl.multiple_of(i * size, size)
        sent[pl.ds(at, size), :] = total[pl.ds(at, size), :]
        kept[pl.ds(at, size), :] = total[pl.ds(half + at, size), :]
        return carry

    lax.fori_loop(0, half // size, give, 0)


def shards(features, block_values, block_rows, block_cols, counts, weight, bias):
    nodes, width = features.shape
    size = block_values.shape[-1]
    per_core = nodes // size
    narrow = lax.axis_size("narrow")
    wide = lax.axis_index("wide")
    values = block_values[0, 0]
    panel = lax.all_to_all(jnp.broadcast_to(features[None], (narrow, nodes, width)), "narrow", 0, 0)
    panel = panel.reshape(narrow * per_core, size, width)
    place = jnp.stack([(wide // (X * CORES)) % SHARE, wide % CORES]).astype(jnp.int32)

    half = Z * X * nodes
    smem = pl.BlockSpec(memory_space=pltpu.SMEM)
    vmem = pl.BlockSpec(memory_space=pltpu.VMEM)
    sent, kept = pl.pallas_call(
        functools.partial(tile_sums, per_core=per_core),
        out_shape=[jax.ShapeDtypeStruct((half, width), jnp.float32)] * 2,
        in_specs=[smem] * 4 + [vmem] * 2,
        out_specs=[vmem] * 2,
        scratch_shapes=[pltpu.VMEM((2 * half, width), jnp.float32)],
        name="tile_sums",
    )(counts.reshape(1), block_rows.reshape(-1), block_cols.reshape(-1), place, values, panel)

    pair = kept + lax.ppermute(sent, "wide", shift(dcore=1))
    pair = pair.reshape(SHARE, RELAYS * X * nodes, width)
    up = lax.ppermute(pair[1].astype(jnp.bfloat16), "wide", shift(dz=1))
    down = lax.ppermute(pair[2].astype(jnp.bfloat16), "wide", shift(dz=-1))
    relayed = pair[0] + up.astype(jnp.float32) + down.astype(jnp.float32)
    relayed = relayed.astype(jnp.bfloat16).reshape(RELAYS * X, nodes, width)
    gathered = lax.all_to_all(relayed, "wide", 0, 0, axis_index_groups=RELAY_GROUPS)
    hidden = jnp.sum(gathered.astype(jnp.float32), axis=0).astype(jnp.bfloat16)
    mixed = jnp.dot(hidden, weight, preferred_element_type=jnp.float32) + bias
    return jnp.maximum(mixed, 0.0).astype(jnp.bfloat16)


def solution(mesh):
    placed = (
        P(("wide", "narrow"), None),
        P("narrow", "wide", None, None, None),
        P("narrow", "wide", None),
        P("narrow", "wide", None),
        P("narrow", "wide"),
        P(),
        P(),
    )
    return jax.shard_map(
        shards, mesh=mesh, in_specs=placed, out_specs=P(("narrow", "wide"), None), check_vma=False
    )
```

```python
import functools

import jax
import jax.numpy as jnp
from jax import lax
from jax.experimental import pallas as pl
from jax.experimental.pallas import tpu as pltpu
from jax.sharding import PartitionSpec as P

Z, X, CORES, SHARE = 12, 2, 2, 3
RELAYS = Z // SHARE
UNROLL = 8


def wide_index(z, x, core):
    return (z % Z) * (X * CORES) + (x % X) * CORES + core % CORES


def pairing(partner):
    return [
        (wide_index(z, x, c), wide_index(*partner(z, x, c)))
        for z in range(Z) for x in range(X) for c in range(CORES)
    ]


OTHER_CORE = pairing(lambda z, x, c: (z, x, 1 - c))
NEAR = pairing(lambda z, x, c: (z + 1 - 2 * (z % 2), x, c))
FAR = pairing(lambda z, x, c: (z - 1 + 2 * (z % 2), x, c))
RELAY_GROUPS = [
    [wide_index(SHARE * q + s, x, c) for q in range(RELAYS) for x in range(X)]
    for s in range(SHARE) for c in range(CORES)
]


def place_of(row, place, per_core):
    core = (row // per_core) % CORES
    x = (row // (per_core * CORES)) % X
    z = row // (per_core * CORES * X)
    relative = lax.rem(place[2] * (z - place[0]) + Z, SHARE)
    inner = (z // SHARE) * (X * per_core) + x * per_core + row % per_core
    return core == place[1], relative * (RELAYS * X * per_core) + inner


def tile_sums(used, rows, cols, place, values, panel, total, picked, where, *, per_core, kept):
    slots, size = values.shape[:2]
    blocks = total.shape[0] // size
    scans = -(-slots // blocks)

    def scan(i, found):
        total[pl.ds(pl.multiple_of(i * size, size), size), :] = jnp.zeros((size, total.shape[1]), jnp.float32)
        for j in range(scans):
            slot = i * scans + j
            ours, at = place_of(rows[slot], place, per_core)
            picked[found] = slot
            where[found] = at
            found = found + jnp.logical_and(ours == kept, slot < used[0]).astype(jnp.int32)
        return found

    found = lax.fori_loop(0, blocks, scan, jnp.int32(0))
    for u in range(UNROLL):
        picked[found + u] = 0
        where[found + u] = 0

    def step(group, carry):
        first = group * UNROLL
        products = []
        for u in range(UNROLL):
            slot = picked[first + u]
            product = jnp.dot(values[slot], panel[cols[slot]], preferred_element_type=jnp.float32)
            products.append(jnp.where(first + u < found, product, 0.0))
        for u in range(UNROLL):
            at = pl.multiple_of(where[first + u] * size, size)
            total[pl.ds(at, size), :] += products[u]
        return carry

    lax.fori_loop(0, (found + UNROLL - 1) // UNROLL, step, 0)


def shards(features, block_values, block_rows, block_cols, counts, weight, bias):
    nodes, width = features.shape
    size = block_values.shape[-1]
    per_core = nodes // size
    narrow = lax.axis_size("narrow")
    wide = lax.axis_index("wide")
    values = block_values[0, 0]
    panel = lax.all_to_all(jnp.broadcast_to(features[None], (narrow, nodes, width)), "narrow", 0, 0)
    panel = panel.reshape(narrow * per_core, size, width)
    z = wide // (X * CORES)
    place = jnp.stack([z % SHARE, wide % CORES, 1 - 2 * (z % 2)]).astype(jnp.int32)

    slots = values.shape[0]
    half = Z * X * nodes
    smem = pl.BlockSpec(memory_space=pltpu.SMEM)
    vmem = pl.BlockSpec(memory_space=pltpu.VMEM)

    def sums(kept):
        return pl.pallas_call(
            functools.partial(tile_sums, per_core=per_core, kept=kept),
            out_shape=pltpu.VMEM((half, width), jnp.float32),
            in_specs=[smem] * 4 + [vmem] * 2,
            out_specs=vmem,
            scratch_shapes=[pltpu.SMEM((slots + UNROLL,), jnp.int32)] * 2,
            compiler_params=pltpu.CompilerParams(vmem_limit_bytes=12 << 20),
            cost_estimate=pl.CostEstimate(
                flops=slots * size * size * width, bytes_accessed=half * width * 4, transcendentals=0
            ),
            name="kept_sums" if kept else "sent_sums",
        )(
            counts.reshape(1), block_rows.reshape(-1), block_cols.reshape(-1), place,
            pltpu.with_memory_space_constraint(values, pltpu.VMEM),
            pltpu.with_memory_space_constraint(panel, pltpu.VMEM),
        )

    received = lax.ppermute(sums(False), "wide", OTHER_CORE)
    kept = sums(True)
    share = RELAYS * X * nodes
    ours, near, far = (
        kept[i * share : (i + 1) * share] + received[i * share : (i + 1) * share] for i in range(SHARE)
    )
    near = lax.ppermute(near.astype(jnp.bfloat16), "wide", NEAR)
    far = lax.ppermute(far.astype(jnp.bfloat16), "wide", FAR)
    relayed = ours + near.astype(jnp.float32) + far.astype(jnp.float32)
    relayed = relayed.astype(jnp.bfloat16).reshape(RELAYS * X, nodes, width)
    gathered = lax.all_to_all(relayed, "wide", 0, 0, axis_index_groups=RELAY_GROUPS)
    hidden = jnp.sum(gathered.astype(jnp.float32), axis=0).astype(jnp.bfloat16)
    mixed = jnp.dot(hidden, weight, preferred_element_type=jnp.float32) + bias
    return jnp.maximum(mixed, 0.0).astype(jnp.bfloat16)


def solution(mesh):
    placed = (
        P(("wide", "narrow"), None),
        P("narrow", "wide", None, None, None),
        P("narrow", "wide", None),
        P("narrow", "wide", None),
        P("narrow", "wide"),
        P(),
        P(),
    )
    return jax.shard_map(
        shards, mesh=mesh, in_specs=placed, out_specs=P(("narrow", "wide"), None), check_vma=False
    )
```

```python
import functools

import jax
import jax.numpy as jnp
from jax import lax
from jax.experimental import pallas as pl
from jax.experimental.pallas import tpu as pltpu
from jax.sharding import PartitionSpec as P

Z, X, CORES, SHARE = 12, 2, 2, 3
RELAYS = Z // SHARE
UNROLL = 8


def wide_index(z, x, core):
    return (z % Z) * (X * CORES) + (x % X) * CORES + core % CORES


def pairing(partner):
    return [
        (wide_index(z, x, c), wide_index(*partner(z, x, c)))
        for z in range(Z) for x in range(X) for c in range(CORES)
    ]


OTHER_CORE = pairing(lambda z, x, c: (z, x, 1 - c))
NEAR = pairing(lambda z, x, c: (z + 1 - 2 * (z % 2), x, c))
FAR = pairing(lambda z, x, c: (z - 1 + 2 * (z % 2), x, c))
LINES, RING = 2, 8
Y_GROUPS = [[x * RING + y for y in range(RING)] for x in range(LINES)]
OTHER_LINE = [(n, (n + RING) % (LINES * RING)) for n in range(LINES * RING)]
RELAY_GROUPS = [
    [wide_index(SHARE * q + s, x, c) for q in range(RELAYS) for x in range(X)]
    for s in range(SHARE) for c in range(CORES)
]


def place_of(row, place, per_core):
    core = (row // per_core) % CORES
    x = (row // (per_core * CORES)) % X
    z = row // (per_core * CORES * X)
    relative = lax.rem(place[2] * (z - place[0]) + Z, SHARE)
    inner = (z // SHARE) * (X * per_core) + x * per_core + row % per_core
    return core == place[1], relative * (RELAYS * X * per_core) + inner


def plan_slots(used, rows, cols, place, plan, sent, kept, *, per_core):
    slots = rows.shape[0]
    blocks = Z * X * per_core
    size = sent.shape[0] // blocks
    line_blocks = RING * per_core
    length = slots + UNROLL
    scans = slots // blocks

    def scan(i, counts):
        at = pl.multiple_of(i * size, size)
        sent[pl.ds(at, size), :] = jnp.zeros((size, sent.shape[1]), jnp.float32)
        kept[pl.ds(at, size), :] = jnp.zeros((size, kept.shape[1]), jnp.float32)
        for j in range(scans):
            slot = i * scans + j
            ours, where = place_of(rows[slot], place, per_core)
            column = cols[slot]
            near = column // line_blocks == place[3]
            chosen = jnp.where(near, 0, 2) + ours.astype(jnp.int32)
            count = counts[3]
            for q in range(3):
                count = jnp.where(chosen == q, counts[q], count)
            entry = 3 * (chosen * length + count)
            plan[entry] = slot
            plan[entry + 1] = where
            plan[entry + 2] = lax.rem(column, line_blocks)
            counts = tuple(
                counts[q] + jnp.logical_and(chosen == q, slot < used[0]).astype(jnp.int32) for q in range(4)
            )
        return counts

    counts = lax.fori_loop(0, blocks, scan, (jnp.int32(0),) * 4)
    for q in range(4):
        plan[3 * 4 * length + q] = counts[q]
        for u in range(3 * UNROLL):
            plan[3 * (q * length + counts[q]) + u] = 0


def tile_sums(plan, values, panel, begun, total, *, which, length):
    size = values.shape[1]
    found = plan[3 * 4 * length + which]

    def step(group, carry):
        first = group * UNROLL
        base = 3 * (which * length + first)
        products = []
        for u in range(UNROLL):
            product = jnp.dot(
                values[plan[base + 3 * u]], panel[plan[base + 3 * u + 2]], preferred_element_type=jnp.float32
            )
            products.append(jnp.where(first + u < found, product, 0.0))
        for u in range(UNROLL):
            at = pl.multiple_of(plan[base + 3 * u + 1] * size, size)
            total[pl.ds(at, size), :] += products[u]
        return carry

    lax.fori_loop(0, (found + UNROLL - 1) // UNROLL, step, 0)


def shards(features, block_values, block_rows, block_cols, counts, weight, bias):
    nodes, width = features.shape
    size = block_values.shape[-1]
    per_core = nodes // size
    wide = lax.axis_index("wide")
    values = block_values[0, 0]
    slots = values.shape[0]
    length = slots + UNROLL
    half = Z * X * nodes
    z = wide // (X * CORES)
    line = lax.axis_index("narrow") // RING
    place = jnp.stack([z % SHARE, wide % CORES, 1 - 2 * (z % 2), line]).astype(jnp.int32)

    smem = pl.BlockSpec(memory_space=pltpu.SMEM)
    vmem = pl.BlockSpec(memory_space=pltpu.VMEM)
    sums_shape = pltpu.VMEM((half, width), jnp.float32)
    plan, sent, kept = pl.pallas_call(
        functools.partial(plan_slots, per_core=per_core),
        out_shape=[jax.ShapeDtypeStruct((3 * 4 * length + 4,), jnp.int32), sums_shape, sums_shape],
        in_specs=[smem] * 4,
        out_specs=[smem, vmem, vmem],
        compiler_params=pltpu.CompilerParams(vmem_limit_bytes=1 << 20),
        cost_estimate=pl.CostEstimate(flops=0, bytes_accessed=half * width * 8, transcendentals=0),
        name="plan_slots",
    )(counts.reshape(1), block_rows.reshape(-1), block_cols.reshape(-1), place)

    values = pltpu.with_memory_space_constraint(values, pltpu.VMEM)

    def add(which, panel, begun):
        panel = panel.reshape(RING * per_core, size, width)
        return pl.pallas_call(
            functools.partial(tile_sums, which=which, length=length),
            out_shape=sums_shape,
            in_specs=[smem] + [vmem] * 3,
            out_specs=vmem,
            input_output_aliases={3: 0},
            compiler_params=pltpu.CompilerParams(vmem_limit_bytes=4 << 20),
            cost_estimate=pl.CostEstimate(
                flops=slots * size * size * width, bytes_accessed=half * width * 4, transcendentals=0
            ),
            name="tile_sums",
        )(plan, values, pltpu.with_memory_space_constraint(panel, pltpu.VMEM), pltpu.with_memory_space_constraint(begun, pltpu.VMEM))

    line_panel = lax.all_to_all(
        jnp.broadcast_to(features[None], (RING, nodes, width)), "narrow", 0, 0, axis_index_groups=Y_GROUPS
    )
    other_panel = lax.ppermute(line_panel, "narrow", OTHER_LINE)
    sent = add(0, line_panel, sent)
    kept = add(1, line_panel, kept)
    other, kept = lax.optimization_barrier((other_panel, kept))
    sent = add(2, other, sent)
    received = lax.ppermute(sent, "wide", OTHER_CORE)
    kept = add(3, other, kept)
    share = RELAYS * X * nodes
    ours, near, far = (
        kept[i * share : (i + 1) * share] + received[i * share : (i + 1) * share] for i in range(SHARE)
    )
    near = lax.ppermute(near.astype(jnp.bfloat16), "wide", NEAR)
    far = lax.ppermute(far.astype(jnp.bfloat16), "wide", FAR)
    relayed = ours + near.astype(jnp.float32) + far.astype(jnp.float32)
    relayed = relayed.astype(jnp.bfloat16).reshape(RELAYS * X, nodes, width)
    gathered = lax.all_to_all(relayed, "wide", 0, 0, axis_index_groups=RELAY_GROUPS)
    hidden = jnp.sum(gathered.astype(jnp.float32), axis=0).astype(jnp.bfloat16)
    mixed = jnp.dot(hidden, weight, preferred_element_type=jnp.float32) + bias
    return jnp.maximum(mixed, 0.0).astype(jnp.bfloat16)


def solution(mesh):
    placed = (
        P(("wide", "narrow"), None),
        P("narrow", "wide", None, None, None),
        P("narrow", "wide", None),
        P("narrow", "wide", None),
        P("narrow", "wide"),
        P(),
        P(),
    )
    return jax.shard_map(
        shards, mesh=mesh, in_specs=placed, out_specs=P(("narrow", "wide"), None), check_vma=False
    )
```
